32 devices in a mesh: groups: 2 (over y), seq: 16 (over z, x, core).
Axes of the slice: x: 2, y: 2, z: 4, core: 2. Of those that a mesh axis runs over, the one named last changes fastest.
Arguments:
- inputs: bfloat16 [16384, 768], P(('groups', 'seq')), parts along dimension 0, may hold values from -6 to 6
- grad_out: bfloat16 [16384, 768], P(('groups', 'seq')), parts along dimension 0, may hold values from -6 to 6
- w_dilated: bfloat16 [3, 768, 384], replicated, may hold values from -0.125 to 0.125
- w_point: bfloat16 [384, 768], replicated, may hold values from -0.3125 to 0.3125
- gain_in: float32 [768], replicated, may hold values from 0.1 to 1.9
- gain_mid: float32 [384], replicated, may hold values from 0.1 to 1.9
- window_lengths: int32 [20], P('groups'), parts along dimension 0, may hold values from 1 to 1536, 8192 in all
Outputs:
- outputs: bfloat16 [16384, 768], P(('groups', 'seq')), parts along dimension 0
- grad_inputs: bfloat16 [16384, 768], P(('groups', 'seq')), parts along dimension 0
- grad_dilated: float32 [6, 768, 384], P('groups', 'seq'), parts along dimension 0
- grad_point: float32 [768, 768], P('groups', 'seq'), parts along dimension 0
- grad_gain_in: float32 [1536], P(('groups', 'seq')), parts along dimension 0
- grad_gain_mid: float32 [768], P(('groups', 'seq')), parts along dimension 0
The draws below stay inside these ranges and needn't reach their ends.
There are 2 independent parts, one for each index of `groups`. The reference program is written for one: setup_inputs(seed, part) draws one part's arguments, and reference() takes and returns one part's arrays. A program takes and returns all parts, laid end to end along the dimension named above; an argument that names none is the same for every part. Nothing has to cross between parts.
Inputs may be any that keep to these rules, and one draw needn't show every extreme that they name: window_lengths sum to 8192 and the longest is exactly 1536.
All inputs are finite; a program needn't handle non-finite values.
Results may differ from the reference program's by a relative error of at most 0.0056.
Values may be sent and summed in bfloat16 or wider, within the bound.
A program may use at most 64 MiB of HBM per device.

```python
import math
import jax
import jax.numpy as jnp
import numpy as np
from jax import lax

C = 768
H = 384
MAXLEN = 1536
DILATION_STEP = 38
TOKENS = 8192
WINDOWS = 10


def strengthened(result, own_key, source, target, shards_of, factor):
    owner, partner = [(jnp.arange(result.shape[dim]) // (result.shape[dim] // shards_of)).reshape([-1 if axis == dim else 1 for axis in range(result.ndim)]) for dim in (source, target)]
    chosen = jax.random.permutation(own_key, shards_of)[partner]
    strong = (owner == chosen) | (owner == (partner + shards_of // 2) % shards_of)
    return jnp.where(strong, factor * result, result)


def shard_levels(key, dims, split, low, top_value):
    factor_of = 1.0
    for dim, blocks in split:
        heights = jax.random.uniform(jax.random.fold_in(jax.random.fold_in(key, 6), dim), (blocks,), jnp.float32, low / len(split), top_value / len(split))
        factor_of = factor_of * jnp.repeat(jnp.exp(heights), dims[dim] // blocks).reshape((-1,) + (1,) * (len(dims) - 1 - dim))
    return factor_of


def profile(number_of, total, most, lean):
    weights = [(1 << 20) // math.isqrt(rank ** lean) + 1 for rank in range(2, number_of + 1)]
    surplus, given = total - most - (number_of - 1), [1] * (number_of - 1)
    while surplus > 0:
        candidates = [i for i in range(number_of - 1) if given[i] < most]
        mass, remaining = sum([weights[i] for i in candidates]), surplus
        for i in candidates:
            more = min(most - given[i], max(1, remaining * weights[i] // mass), surplus)
            given[i] = given[i] + more
            surplus = surplus - more
    return np.array([most] + given)


def ragged(rng, amount, total, limit, slope):
    if amount == 2:
        one = jax.random.randint(rng, (), max(1, total - limit), min(limit, total - 1) + 1)
        return jnp.stack([one, total - one])
    lengths = jnp.asarray(profile(amount, total, limit, slope), jnp.int32)
    couples = (amount - 1) // 2
    giver, receiver = lengths[1:1 + 2 * couples:2], lengths[2:2 + 2 * couples:2]
    room = jnp.minimum(giver - 1, limit - receiver)
    shifted = jax.random.randint(jax.random.fold_in(rng, 1), (couples,), 0, 1 << 20) % (room + 1)
    lengths = lengths.at[1:1 + 2 * couples:2].set(giver - shifted).at[2:2 + 2 * couples:2].set(receiver + shifted)
    return lengths[jax.random.permutation(jax.random.fold_in(rng, 2), amount)]


def bell_draw(rng, shape, width, limit, pieces=(), kind=jnp.bfloat16):
    result = jax.random.normal(rng, shape, jnp.float32) * width
    if len(pieces) > 0:
        result = shard_levels(rng, shape, pieces, -0.22, 0.18) * result
    return jnp.clip(result, min=-limit, max=limit).astype(kind)


def gaussian_with(own_key, extent, spread, bound, cuts, heavy, kind=jnp.bfloat16):
    result = spread * jax.random.normal(own_key, extent, jnp.float32)
    if cuts:
        result = result * shard_levels(own_key, extent, cuts, -0.22, 0.18)
    return jnp.clip(strengthened(result, jax.random.fold_in(own_key, 3), *heavy), -bound, bound).astype(kind)


def setup_inputs(seed: int = 0, part: int = 0) -> dict:
    streams_of = jax.random.split(jax.random.key(seed), 8)
    own_keys = jax.random.split(jax.random.fold_in(streams_of[7], part), 8)
    return {
        "inputs": gaussian_with(own_keys[0], (TOKENS, C), 1.0, 6.0, ((0, 16),), (0, 1, 16, 2.0)),
        "grad_out": gaussian_with(own_keys[1], (TOKENS, C), 1.0, 6.0, ((0, 16),), (0, 1, 16, 2.0)),
        "w_dilated": bell_draw(streams_of[2], (3, C, H), (3 * C) ** -0.5, 0.125),
        "w_point": bell_draw(streams_of[3], (H, C), H ** -0.5, 0.3125),
        "gain_in": jnp.clip(1.0 + 0.18 * jax.random.normal(streams_of[4], (C,), jnp.float32), 0.1, 1.9),
        "gain_mid": jnp.clip(1.0 + 0.18 * jax.random.normal(streams_of[5], (H,), jnp.float32), 0.1, 1.9),
        "window_lengths": ragged(own_keys[6], WINDOWS, TOKENS, MAXLEN, 2).astype(jnp.int32),
    }


def norm_gelu(values, gain):
    scale = lax.rsqrt(lax.optimization_barrier(jnp.mean(values * values, axis=-1, keepdims=True)) + 1e-06)
    return jax.nn.gelu(values * scale * gain, approximate=True)

def window_ids(bin_positions, window_lengths):
    bounds = jnp.cumsum(window_lengths).astype(jnp.int32)
    window_labels = lax.optimization_barrier(jnp.sum((bin_positions[:, None] >= bounds[None, :]).astype(jnp.int32), axis=1)).astype(jnp.int32)
    return jnp.where(bin_positions < 0, -1, window_labels).astype(jnp.int32)

def reference(inputs, grad_out, w_dilated, w_point, gain_in, gain_mid, window_lengths):
    total_length = inputs.shape[0]
    channel_count = inputs.shape[1]
    hidden_channels = w_point.shape[0]
    bin_positions = jnp.arange(-DILATION_STEP, total_length + DILATION_STEP, dtype=jnp.int32)
    window_labels = window_ids(bin_positions, window_lengths)
    middle_tap = window_labels[DILATION_STEP:DILATION_STEP + total_length]
    mask_lo = (window_labels[:total_length] == middle_tap).astype(jnp.bfloat16)[:, None]
    upper_mask = (window_labels[2 * DILATION_STEP:] == middle_tap).astype(jnp.bfloat16)[:, None]
    inputs_f = inputs.astype(jnp.float32)
    input_activation = norm_gelu(inputs_f, gain_in).astype(jnp.bfloat16)
    zeroed_border = jnp.zeros((DILATION_STEP, channel_count), jnp.bfloat16)
    padded_input = jnp.concatenate([zeroed_border, input_activation, zeroed_border], axis=0)
    u_lo = padded_input[:total_length] * mask_lo
    upper_preactivation = padded_input[2 * DILATION_STEP:] * upper_mask
    hidden = jnp.dot(u_lo, w_dilated[0], preferred_element_type=jnp.float32) + jnp.dot(input_activation, w_dilated[1], preferred_element_type=jnp.float32) + jnp.dot(upper_preactivation, w_dilated[2], preferred_element_type=jnp.float32)
    act_mid, vjp_mid = jax.vjp(norm_gelu, hidden, gain_mid)
    act_mid = act_mid.astype(jnp.bfloat16)
    outputs = (inputs_f + jnp.dot(act_mid, w_point, preferred_element_type=jnp.float32)).astype(jnp.bfloat16)
    grad_mid = jnp.dot(grad_out, w_point.T, preferred_element_type=jnp.float32)
    grad_point = jnp.dot(act_mid.T, grad_out, preferred_element_type=jnp.float32)
    grad_hidden_f, grad_gain_mid = vjp_mid(grad_mid)
    hidden_gradient = grad_hidden_f.astype(jnp.bfloat16)
    zeroed_gradient = jnp.zeros((DILATION_STEP, hidden_channels), jnp.bfloat16)
    padded_gradient = jnp.concatenate([zeroed_gradient, hidden_gradient, zeroed_gradient], axis=0)
    grad_lo = padded_gradient[:total_length] * mask_lo
    upper_gradient = padded_gradient[2 * DILATION_STEP:] * upper_mask
    grad_act = jnp.dot(upper_gradient, w_dilated[0].T, preferred_element_type=jnp.float32) + jnp.dot(hidden_gradient, w_dilated[1].T, preferred_element_type=jnp.float32) + jnp.dot(grad_lo, w_dilated[2].T, preferred_element_type=jnp.float32)
    grad_dilated = jnp.stack([jnp.dot(u_lo.T, hidden_gradient, preferred_element_type=jnp.float32), jnp.dot(input_activation.T, hidden_gradient, preferred_element_type=jnp.float32), jnp.dot(upper_preactivation.T, hidden_gradient, preferred_element_type=jnp.float32)], axis=0)
    _, vjp_in = jax.vjp(norm_gelu, inputs_f, gain_in)
    grad_branch, grad_gain_in = vjp_in(grad_act)
    grad_inputs = (grad_out.astype(jnp.float32) + grad_branch).astype(jnp.bfloat16)
    return (outputs, grad_inputs, grad_dilated, grad_point, grad_gain_in, grad_gain_mid)
```

```python
import functools

import jax
import jax.numpy as jnp
from jax import lax
from jax.experimental import pallas as pl
from jax.experimental.pallas import tpu as pltpu
from jax.sharding import PartitionSpec as P

STEP = 38
XH = 96
GH = 48
EPS = 1e-06
K0 = 0.7978845608028654
K1 = 0.044715
F32 = jnp.float32
BF16 = jnp.bfloat16
NT = (((1,), (1,)), ((), ()))


def dot(a, b):
    return jnp.dot(a, b, preferred_element_type=F32)


def dot_nt(a, b):
    return lax.dot_general(a, b, NT, preferred_element_type=F32)


def gelu_parts(a):
    sq = a * a
    th = jnp.tanh(a * (K0 + (K0 * K1) * sq))
    half = 0.5 + 0.5 * th
    slope = half + a * (half * (1.0 - th)) * (K0 + (3.0 * K0 * K1) * sq)
    return a * half, slope


def scale_of(z):
    return lax.rsqrt(jnp.mean(z * z, axis=-1, keepdims=True) + EPS)


def fold(p):
    return jnp.sum(p.reshape(p.shape[0] // 8, 8, p.shape[1]), axis=0)


def kernel(n, levels, x_ref, g_ref, wd_ref, wp_ref, gin_ref, gmid_ref, b_ref,
           out_ref, gi_ref, shard_ref, gains_ref,
           xh, gh, u_ref, gp_ref, h_ref, dv_ref, v_ref, dh_ref, dd_ref, du_ref,
           tmp, lt, mlo, mhi, acc, gacc, gs, gr, hs, hr, gss, grs, ss, rs, *bufs):
    rows, c = x_ref.shape
    hid = gmid_ref.shape[1]
    ext = rows + 2 * GH
    me = lax.axis_index("seq")
    left, right = (me + n - 1) % n, (me + 1) % n
    send, recv = bufs[:levels], bufs[levels:]
    bit = [(me // 2**k) % 2 for k in range(levels)]
    partner = [me + (1 - 2 * bit[k]) * 2**k for k in range(levels)]

    barrier = pltpu.get_barrier_semaphore()
    peers = [left, right] + partner
    for p in peers:
        pl.semaphore_signal(barrier, inc=1, device_id={"seq": p}, device_id_type=pl.DeviceIdType.MESH)
    pl.semaphore_wait(barrier, len(peers))

    def remote(src, dst, s, r, to):
        return pltpu.make_async_remote_copy(
            src_ref=src, dst_ref=dst, send_sem=s, recv_sem=r,
            device_id={"seq": to}, device_id_type=pl.DeviceIdType.MESH)

    up = [remote(x_ref.at[rows - XH:rows], xh.at[0], hs.at[0], hr.at[0], right),
          remote(g_ref.at[rows - GH:rows], gh.at[0], hs.at[1], hr.at[1], right)]
    down = [remote(x_ref.at[0:XH], xh.at[1], hs.at[2], hr.at[2], left),
            remote(g_ref.at[0:GH], gh.at[1], hs.at[3], hr.at[3], left)]

    @pl.when(me < n - 1)
    def _():
        for d in up:
            d.start()

    @pl.when(me > 0)
    def _():
        for d in down:
            d.start()

    @pl.when(me == 0)
    def _():
        xh[0] = jnp.zeros((XH, c), BF16)
        gh[0] = jnp.zeros((GH, c), BF16)

    @pl.when(me == n - 1)
    def _():
        xh[1] = jnp.zeros((XH, c), BF16)
        gh[1] = jnp.zeros((GH, c), BF16)

    gin = gin_ref[...]
    gmid = gmid_ref[...]

    def act_own(i, carry):
        at = pl.multiple_of(i * 32, 32)
        z = x_ref[pl.ds(at, 32), :].astype(F32)
        u, slope = gelu_parts(z * scale_of(z) * gin)
        u_ref[pl.ds(XH + at, 32), :] = u.astype(BF16)
        gp_ref[pl.ds(at, 32), :] = slope
        return carry

    lax.fori_loop(0, rows // 32, act_own, 0)
    dv_ref[GH:GH + rows, :] = dot_nt(g_ref[...], wp_ref[...])

    b = b_ref[...]
    t = me * rows - GH + lax.broadcasted_iota(jnp.int32, (ext, b.shape[1]), 0)
    cut_lo = jnp.where((b > t - STEP) & (b <= t), 1.0, 0.0)
    cut_hi = jnp.where((b > t) & (b <= t + STEP), 1.0, 0.0)
    mlo[...] = 1.0 - jnp.max(cut_lo, axis=1, keepdims=True)
    mhi[...] = 1.0 - jnp.max(cut_hi, axis=1, keepdims=True)

    chunk = c // n if levels else c
    def transposed(j, value):
        if not levels:
            lt[j] = value.T
            return
        tmp[...] = value.T.reshape(n, chunk, rows)
        for s in range(n):
            at = 0
            for k in range(levels):
                flip = (s >> (levels - 1 - k)) & 1
                at = at + (1 - bit[k] if flip else bit[k]) * 2**k
            lt[j, s * chunk:(s + 1) * chunk] = tmp[at]

    transposed(0, g_ref[...])
    transposed(1, u_ref[XH:XH + rows, :])

    @pl.when(me > 0)
    def _():
        for d in up:
            d.wait_recv()

    @pl.when(me < n - 1)
    def _():
        for d in down:
            d.wait_recv()

    for side, base in ((0, 0), (1, XH + rows)):
        for i in range(XH // 32):
            z = xh[side, i * 32:(i + 1) * 32, :].astype(F32)
            u, _ = gelu_parts(z * scale_of(z) * gin)
            u_ref[base + i * 32:base + (i + 1) * 32, :] = u.astype(BF16)
    dv_ref[0:GH, :] = dot_nt(gh[0], wp_ref[...])
    dv_ref[GH + rows:ext, :] = dot_nt(gh[1], wp_ref[...])

    off = XH - GH
    tile = ext // 2
    for q in range(0, ext, tile):
        at = off + q
        low = dot(u_ref[at - STEP:at - STEP + tile, :], wd_ref[0])
        mid = dot(u_ref[at:at + tile, :], wd_ref[1])
        high = dot(u_ref[at + STEP:at + STEP + tile, :], wd_ref[2])
        h_ref[q:q + tile, :] = low * mlo[q:q + tile, :] + mid + high * mhi[q:q + tile, :]

    def middle(at, size):
        z = h_ref[pl.ds(at, size), :]
        r = scale_of(z)
        nz = z * r
        v, slope = gelu_parts(nz * gmid)
        da = dv_ref[pl.ds(at, size), :] * slope
        dn = da * gmid
        dz = r * (dn - nz * jnp.mean(dn * nz, axis=-1, keepdims=True))
        v_ref[pl.ds(at, size), :] = v.astype(BF16)
        dh_ref[pl.ds(at, size), :] = dz.astype(BF16)
        return da * nz

    middle(0, GH)
    middle(GH + rows, GH)
    gain_mid = lax.fori_loop(
        0, rows // 64,
        lambda i, a: a + fold(middle(pl.multiple_of(GH + i * 64, 16), 64)),
        jnp.zeros((8, hid), F32))

    step = {}

    def start(m, k):
        step[m, k] = remote(send[k].at[m], recv[k].at[m], ss.at[m * levels + k], rs.at[m * levels + k], partner[k])
        step[m, k].start()

    def share(m, left_t, right_m):
        if not levels:
            shard_ref[m] = dot(left_t[...], right_m)
            return
        half = c // 2
        send[0][m] = dot(left_t[half:c, :], right_m).astype(BF16)
        start(m, 0)
        acc[m] = dot(left_t[0:half, :], right_m)

    def advance(m, k):
        if not levels:
            return
        size = c >> (k + 1)
        step[m, k].wait_recv()
        if k == levels - 1:
            shard_ref[m] = acc[m, 0:size, :] + recv[k][m].astype(F32)
            return
        half = size // 2
        send[k + 1][m] = (acc[m, half:size, :] + recv[k][m, half:size, :].astype(F32)).astype(BF16)
        start(m, k + 1)
        acc[m, 0:half, :] = acc[m, 0:half, :] + recv[k][m, 0:half, :].astype(F32)

    def wave(i):
        for m in range(4):
            if 0 <= i - m < levels:
                advance(m, i - m)

    share(0, lt.at[0], v_ref[GH:GH + rows, :])
    own = slice(GH, GH + rows)
    dd_ref[0] = (dh_ref[GH + STEP:GH + STEP + rows, :].astype(F32) * mhi[own, :]).astype(BF16)
    share(1, lt.at[1], dd_ref[0])
    wave(0)
    dd_ref[1] = dh_ref[own, :]
    share(2, lt.at[1], dd_ref[1])
    if levels:
        advance(1, 0)
    dd_ref[2] = (dh_ref[GH - STEP:GH - STEP + rows, :].astype(F32) * mlo[own, :]).astype(BF16)
    share(3, lt.at[1], dd_ref[2])
    if levels:
        advance(2, 0)

    def cotangent(q, size):
        du_ref[q:q + size, :] = (dot_nt(dd_ref[0, q:q + size, :], wd_ref[0])
                                 + dot_nt(dd_ref[1, q:q + size, :], wd_ref[1])
                                 + dot_nt(dd_ref[2, q:q + size, :], wd_ref[2]))

    def back(i, a):
        at = pl.multiple_of(i * 32, 32)
        z = x_ref[pl.ds(at, 32), :].astype(F32)
        r = scale_of(z)
        nz = z * r
        da = du_ref[pl.ds(at, 32), :] * gp_ref[pl.ds(at, 32), :]
        dn = da * gin
        dz = r * (dn - nz * jnp.mean(dn * nz, axis=-1, keepdims=True))
        gi_ref[pl.ds(at, 32), :] = (g_ref[pl.ds(at, 32), :].astype(F32) + dz).astype(BF16)
        return a + fold(da * nz)

    half_rows = rows // 2
    gain_in = jnp.zeros((8, c), F32)
    cotangent(0, half_rows)
    if levels:
        advance(3, 0)
        advance(0, 1)
    gain_in = lax.fori_loop(0, half_rows // 32, back, gain_in)
    if levels:
        advance(1, 1)
        advance(0, 2)
    cotangent(half_rows, half_rows)
    gain_in = lax.fori_loop(half_rows // 32, rows // 32, back, gain_in)

    if not levels:
        gains_ref[:, 0:c] = gain_in
        gains_ref[:, c:c + hid] = gain_mid
    else:
        gacc[:, 0:c] = gain_in
        gacc[:, c:c + hid] = gain_mid
    gains = {}

    def gain_start(k):
        if levels:
            gs[k] = gacc[...]
            gains[k] = remote(gs.at[k], gr.at[k], gss.at[k], grs.at[k], partner[k])
            gains[k].start()

    def gain_end(k):
        if levels:
            gains[k].wait_recv()
            gacc[...] = gacc[...] + gr[k]

    gain_start(0)
    for q in range(0, rows, half_rows):
        s = slice(q, q + half_rows)
        y = dot(v_ref[GH + q:GH + q + half_rows, :], wp_ref[...])
        out_ref[s, :] = (x_ref[s, :].astype(F32) + y).astype(BF16)
    if levels:
        done = {(0, 0), (1, 0), (2, 0), (3, 0), (0, 1), (1, 1), (0, 2)}
        order = [(m, k) for i in range(levels + 3) for m in range(4) for k in (i - m,)
                 if 0 <= k < levels and (m, k) not in done]
        pending = 0
        for j, (m, k) in enumerate(order):
            advance(m, k)
            if j % 2 == 1 and pending < levels:
                gain_end(pending)
                pending += 1
                if pending < levels:
                    gain_start(pending)
        while pending < levels:
            gain_end(pending)
            pending += 1
            if pending < levels:
                gain_start(pending)
        gains_ref[...] = gacc[...]
        for d in list(step.values()) + list(gains.values()):
            d.wait_send()

    @pl.when(me < n - 1)
    def _():
        for d in up:
            d.wait_send()

    @pl.when(me > 0)
    def _():
        for d in down:
            d.wait_send()


def per_device(n, inputs, grad_out, w_dilated, w_point, gain_in, gain_mid, window_lengths):
    rows, c = inputs.shape
    hid = gain_mid.shape[0]
    levels = n.bit_length() - 1 if n & (n - 1) == 0 and c % (16 * n) == 0 else 0
    ext = rows + 2 * GH
    count = window_lengths.shape[0]
    lanes = -(-(count + 1) // 128) * 128
    lane = lax.broadcasted_iota(jnp.int32, (count, lanes), 1)
    index = lax.broadcasted_iota(jnp.int32, (count, lanes), 0)
    bounds = jnp.sum(jnp.where(index < lane, window_lengths[:, None], 0), axis=0, keepdims=True)
    shard = (4, c // n, hid) if levels else (4, c, hid)
    slots = [(4, c >> (k + 1), hid) for k in range(levels)]
    sems = max(levels, 1)
    vmem = pltpu.VMEM
    dma = pltpu.SemaphoreType.DMA
    gain_slots = (sems, 8, c + hid)
    out, gin, shares, gains = pl.pallas_call(
        functools.partial(kernel, n, levels),
        out_shape=(
            jax.ShapeDtypeStruct((rows, c), BF16),
            jax.ShapeDtypeStruct((rows, c), BF16),
            jax.ShapeDtypeStruct(shard, F32),
            jax.ShapeDtypeStruct((8, c + hid), F32),
        ),
        in_specs=[pl.BlockSpec(memory_space=vmem)] * 7,
        out_specs=[pl.BlockSpec(memory_space=vmem)] * 4,
        scratch_shapes=[
            vmem((2, XH, c), BF16), vmem((2, GH, c), BF16), vmem((rows + 2 * XH, c), BF16),
            vmem((rows, c), F32), vmem((ext, hid), F32), vmem((ext, hid), F32),
            vmem((ext, hid), BF16), vmem((ext, hid), BF16), vmem((3, rows, hid), BF16),
            vmem((rows, c), F32),
            vmem((n, c // n, rows) if levels else (8, 128), BF16), vmem((2, c, rows), BF16),
            vmem((ext, 1), F32), vmem((ext, 1), F32),
            vmem((4, c // 2, hid) if levels else (8, 128), F32), vmem((8, c + hid), F32),
            vmem(gain_slots, F32), vmem(gain_slots, F32),
            dma((4,)), dma((4,)), dma((sems,)), dma((sems,)), dma((4 * sems,)), dma((4 * sems,)),
        ] + [vmem(s, BF16) for s in slots] * 2,
        compiler_params=pltpu.CompilerParams(
            collective_id=0, has_side_effects=True, vmem_limit_bytes=48 * 2**20),
        cost_estimate=pl.CostEstimate(flops=12 * rows * c * hid, bytes_accessed=10 * rows * c, transcendentals=0),
    )(inputs, grad_out, w_dilated, w_point, gain_in[None, :], gain_mid[None, :], bounds)
    me = lax.axis_index("seq")
    if levels:
        total = jnp.sum(gains, axis=0)
        own_in = lax.dynamic_slice_in_dim(total[:c], me * (c // n), c // n)
        own_mid = lax.dynamic_slice_in_dim(total[c:], me * (hid // n), hid // n)
    else:
        shares = lax.psum_scatter(shares, "seq", scatter_dimension=1, tiled=True)
        total = jnp.sum(gains, axis=0)
        own_in = lax.psum_scatter(total[:c], "seq", scatter_dimension=0, tiled=True)
        own_mid = lax.psum_scatter(total[c:], "seq", scatter_dimension=0, tiled=True)
    return out, gin, shares[1:], shares[0].T, own_in, own_mid


def solution(mesh):
    rows = P(("groups", "seq"), None)
    vector = P(("groups", "seq"))
    return jax.shard_map(
        functools.partial(per_device, mesh.shape["seq"]),
        mesh=mesh,
        in_specs=(rows, rows, P(), P(), P(), P(), P("groups")),
        out_specs=(rows, rows, P("groups", "seq", None), P("groups", "seq"), vector, vector),
        check_vma=False,
    )
```

```python
import functools

import jax
import jax.numpy as jnp
from jax import lax
from jax.experimental import pallas as pl
from jax.experimental.pallas import tpu as pltpu
from jax.sharding import PartitionSpec as P

STEP = 38
XH = 96
GH = 48
EPS = 1e-06
K0 = 0.7978845608028654
K1 = 0.044715
F32 = jnp.float32
BF16 = jnp.bfloat16
NT = (((1,), (1,)), ((), ()))


def dot(a, b):
    return jnp.dot(a, b, preferred_element_type=F32)


def dot_nt(a, b):
    return lax.dot_general(a, b, NT, preferred_element_type=F32)


def gelu_parts(a):
    sq = a * a
    th = jnp.tanh(a * (K0 + (K0 * K1) * sq))
    half = 0.5 + 0.5 * th
    slope = half + a * (half * (1.0 - th)) * (K0 + (3.0 * K0 * K1) * sq)
    return a * half, slope


def scale_of(z):
    return lax.rsqrt(jnp.mean(z * z, axis=-1, keepdims=True) + EPS)


def fold(p):
    return jnp.sum(p.reshape(p.shape[0] // 8, 8, p.shape[1]), axis=0)


def kernel(n, levels, x_hbm, g_hbm, wd_hbm, wp_hbm, gin_ref, gmid_ref, len_ref,
           out_ref, gi_ref, shard_ref, gains_ref,
           x_ref, g_ref, wd_ref, wp_ref, ls, xh, gh, u_ref, gp_ref, h_ref, dv_ref, v_ref, dh_ref, dd_ref, du_ref,
           tmp, lt, mlo, mhi, acc, gacc, gs, gr, hs, hr, gss, grs, ss, rs, *bufs):
    rows, c = x_ref.shape
    hid = gmid_ref.shape[0]
    ext = rows + 2 * GH
    me = lax.axis_index("seq")
    left, right = (me + n - 1) % n, (me + 1) % n
    send, recv = bufs[:levels], bufs[levels:]
    bit = [(me // 2**k) % 2 for k in range(levels)]
    partner = [me + (1 - 2 * bit[k]) * 2**k for k in range(levels)]

    loads = [pltpu.make_async_copy(a, b, ls.at[i]) for i, (a, b) in enumerate(
        ((x_hbm, x_ref), (g_hbm, g_ref), (wp_hbm, wp_ref), (wd_hbm, wd_ref)))]
    for d in loads:
        d.start()
    barrier = pltpu.get_barrier_semaphore()
    peers = [left, right] + partner
    for p in peers:
        pl.semaphore_signal(barrier, inc=1, device_id={"seq": p}, device_id_type=pl.DeviceIdType.MESH)
    pl.semaphore_wait(barrier, len(peers))

    def remote(src, dst, s, r, to):
        return pltpu.make_async_remote_copy(
            src_ref=src, dst_ref=dst, send_sem=s, recv_sem=r,
            device_id={"seq": to}, device_id_type=pl.DeviceIdType.MESH)

    up = [remote(x_hbm.at[rows - XH:rows], xh.at[0], hs.at[0], hr.at[0], right),
          remote(g_hbm.at[rows - GH:rows], gh.at[0], hs.at[1], hr.at[1], right)]
    down = [remote(x_hbm.at[0:XH], xh.at[1], hs.at[2], hr.at[2], left),
            remote(g_hbm.at[0:GH], gh.at[1], hs.at[3], hr.at[3], left)]

    @pl.when(me < n - 1)
    def _():
        for d in up:
            d.start()

    @pl.when(me > 0)
    def _():
        for d in down:
            d.start()

    @pl.when(me == 0)
    def _():
        xh[0] = jnp.zeros((XH, c), BF16)
        gh[0] = jnp.zeros((GH, c), BF16)

    @pl.when(me == n - 1)
    def _():
        xh[1] = jnp.zeros((XH, c), BF16)
        gh[1] = jnp.zeros((GH, c), BF16)

    gin = gin_ref[...].reshape(1, c)
    gmid = gmid_ref[...].reshape(1, hid)
    loads[0].wait()

    def act_own(i, carry):
        at = pl.multiple_of(i * 32, 32)
        z = x_ref[pl.ds(at, 32), :].astype(F32)
        u, slope = gelu_parts(z * scale_of(z) * gin)
        u_ref[pl.ds(XH + at, 32), :] = u.astype(BF16)
        gp_ref[pl.ds(at, 32), :] = slope
        return carry

    lax.fori_loop(0, rows // 32, act_own, 0)
    loads[1].wait()
    loads[2].wait()
    dv_ref[GH:GH + rows, :] = dot_nt(g_ref[...], wp_ref[...])

    count = len_ref.shape[0]
    lanes = -(-(count + 1) // 128) * 128
    lane = lax.broadcasted_iota(jnp.int32, (8, lanes), 1)
    b = jnp.zeros((8, lanes), jnp.int32)
    for w in range(count):
        b = b + jnp.where(lane > w, len_ref[w], 0)
    b = b[0:1, :]
    t = me * rows - GH + lax.broadcasted_iota(jnp.int32, (ext, b.shape[1]), 0)
    cut_lo = jnp.where((b > t - STEP) & (b <= t), 1.0, 0.0)
    cut_hi = jnp.where((b > t) & (b <= t + STEP), 1.0, 0.0)
    mlo[...] = 1.0 - jnp.max(cut_lo, axis=1, keepdims=True)
    mhi[...] = 1.0 - jnp.max(cut_hi, axis=1, keepdims=True)

    chunk = c // n if levels else c
    def transposed(j, value):
        if not levels:
            lt[j] = value.T
            return
        tmp[...] = value.T.reshape(n, chunk, rows)
        for s in range(n):
            at = 0
            for k in range(levels):
                flip = (s >> (levels - 1 - k)) & 1
                at = at + (1 - bit[k] if flip else bit[k]) * 2**k
            lt[j, s * chunk:(s + 1) * chunk] = tmp[at]

    transposed(0, g_ref[...])
    transposed(1, u_ref[XH:XH + rows, :])

    @pl.when(me > 0)
    def _():
        for d in up:
            d.wait_recv()

    @pl.when(me < n - 1)
    def _():
        for d in down:
            d.wait_recv()

    for side, base in ((0, 0), (1, XH + rows)):
        for i in range(XH // 32):
            z = xh[side, i * 32:(i + 1) * 32, :].astype(F32)
            u, _ = gelu_parts(z * scale_of(z) * gin)
            u_ref[base + i * 32:base + (i + 1) * 32, :] = u.astype(BF16)
    dv_ref[0:GH, :] = dot_nt(gh[0], wp_ref[...])
    dv_ref[GH + rows:ext, :] = dot_nt(gh[1], wp_ref[...])

    loads[3].wait()
    off = XH - GH
    tile = ext // 2
    for q in range(0, ext, tile):
        at = off + q
        low = dot(u_ref[at - STEP:at - STEP + tile, :], wd_ref[0])
        mid = dot(u_ref[at:at + tile, :], wd_ref[1])
        high = dot(u_ref[at + STEP:at + STEP + tile, :], wd_ref[2])
        h_ref[q:q + tile, :] = low * mlo[q:q + tile, :] + mid + high * mhi[q:q + tile, :]

    def middle(at, size):
        z = h_ref[pl.ds(at, size), :]
        r = scale_of(z)
        nz = z * r
        v, slope = gelu_parts(nz * gmid)
        da = dv_ref[pl.ds(at, size), :] * slope
        dn = da * gmid
        dz = r * (dn - nz * jnp.mean(dn * nz, axis=-1, keepdims=True))
        v_ref[pl.ds(at, size), :] = v.astype(BF16)
        dh_ref[pl.ds(at, size), :] = dz.astype(BF16)
        return da * nz

    middle(0, GH)
    middle(GH + rows, GH)
    gain_mid = lax.fori_loop(
        0, rows // 64,
        lambda i, a: a + fold(middle(pl.multiple_of(GH + i * 64, 16), 64)),
        jnp.zeros((8, hid), F32))

    swap = levels == 4
    paths = [list(range(levels)) for _ in range(4)]
    if swap:
        paths[3] = [0, 2, 1, 3]
    step = {}

    def start(m, k):
        step[m, k] = remote(send[k].at[m], recv[k].at[m], ss.at[m * levels + k], rs.at[m * levels + k], partner[paths[m][k]])
        step[m, k].start()

    def share(m, left_t, right_m):
        if not levels:
            shard_ref[m] = dot(left_t[...], right_m)
            return
        half = c // 2
        quarter = half // 4
        places = [0, 2, 1, 3] if swap and m == 3 else [0, 1, 2, 3]
        far = dot(left_t[half:c, :], right_m).astype(BF16)
        for i, j in enumerate(places):
            send[0][m, i * quarter:(i + 1) * quarter, :] = far[j * quarter:(j + 1) * quarter, :]
        start(m, 0)
        near = dot(left_t[0:half, :], right_m)
        for i, j in enumerate(places):
            acc[m, i * quarter:(i + 1) * quarter, :] = near[j * quarter:(j + 1) * quarter, :]

    def advance(m, k):
        if not levels:
            return
        size = c >> (k + 1)
        step[m, k].wait_recv()
        if k == levels - 1:
            shard_ref[m] = acc[m, 0:size, :] + recv[k][m].astype(F32)
            return
        half = size // 2
        send[k + 1][m] = (acc[m, half:size, :] + recv[k][m, half:size, :].astype(F32)).astype(BF16)
        start(m, k + 1)
        acc[m, 0:half, :] = acc[m, 0:half, :] + recv[k][m, 0:half, :].astype(F32)

    def wave(i):
        for m in range(4):
            if 0 <= i - m < levels:
                advance(m, i - m)

    share(0, lt.at[0], v_ref[GH:GH + rows, :])
    own = slice(GH, GH + rows)
    dd_ref[0] = (dh_ref[GH + STEP:GH + STEP + rows, :].astype(F32) * mhi[own, :]).astype(BF16)
    share(1, lt.at[1], dd_ref[0])
    wave(0)
    dd_ref[1] = dh_ref[own, :]
    share(2, lt.at[1], dd_ref[1])
    if levels:
        advance(1, 0)
    dd_ref[2] = (dh_ref[GH - STEP:GH - STEP + rows, :].astype(F32) * mlo[own, :]).astype(BF16)
    share(3, lt.at[1], dd_ref[2])
    if levels:
        advance(2, 0)

    def cotangent(q, size):
        du_ref[q:q + size, :] = (dot_nt(dd_ref[0, q:q + size, :], wd_ref[0])
                                 + dot_nt(dd_ref[1, q:q + size, :], wd_ref[1])
                                 + dot_nt(dd_ref[2, q:q + size, :], wd_ref[2]))

    def back(i, a):
        at = pl.multiple_of(i * 32, 32)
        z = x_ref[pl.ds(at, 32), :].astype(F32)
        r = scale_of(z)
        nz = z * r
        da = du_ref[pl.ds(at, 32), :] * gp_ref[pl.ds(at, 32), :]
        dn = da * gin
        dz = r * (dn - nz * jnp.mean(dn * nz, axis=-1, keepdims=True))
        gi_ref[pl.ds(at, 32), :] = (g_ref[pl.ds(at, 32), :].astype(F32) + dz).astype(BF16)
        return a + fold(da * nz)

    gains = {}

    def gain_start(k):
        if levels:
            gs[k] = gacc[...]
            gains[k] = remote(gs.at[k], gr.at[k], gss.at[k], grs.at[k], partner[k])
            gains[k].start()

    def gain_end(k):
        if levels:
            gains[k].wait_recv()
            gacc[...] = gacc[...] + gr[k]

    def output(q, size):
        y = dot(v_ref[GH + q:GH + q + size, :], wp_ref[...])
        out_ref[q:q + size, :] = (x_ref[q:q + size, :].astype(F32) + y).astype(BF16)

    half_rows = rows // 2
    quarter_rows = rows // 4
    advanced = {(0, 0), (1, 0), (2, 0)}

    def go(*pairs):
        for m, k in pairs:
            if k < levels and (m, k) not in advanced:
                advance(m, k)
                advanced.add((m, k))

    gain_in = jnp.zeros((8, c), F32)
    cotangent(0, half_rows)
    go((3, 0))
    cotangent(half_rows, half_rows)
    go((0, 1))
    gain_in = lax.fori_loop(0, half_rows // 32, back, gain_in)
    go((3, 1), (1, 1), (0, 2))
    gain_in = lax.fori_loop(half_rows // 32, rows // 32, back, gain_in)
    if not levels:
        gains_ref[:, 0:c] = gain_in
        gains_ref[:, c:c + hid] = gain_mid
    else:
        gacc[:, 0:c] = gain_in
        gacc[:, c:c + hid] = gain_mid
    gain_start(0)
    go((2, 1), (1, 2), (0, 3), (3, 2))
    output(0, half_rows)
    if levels:
        gain_end(0)
        for k in range(1, levels):
            gain_start(k)
            if k == 1:
                go((1, 3), (2, 2))
                output(half_rows, half_rows)
            if k == 2:
                go((3, 3), (2, 3))
            gain_end(k)
        go(*[(m, k) for k in range(levels) for m in range(4)])
        gains_ref[...] = gacc[...]
        for d in list(step.values()) + list(gains.values()):
            d.wait_send()
    if levels < 2:
        output(half_rows, half_rows)

    @pl.when(me < n - 1)
    def _():
        for d in up:
            d.wait_send()

    @pl.when(me > 0)
    def _():
        for d in down:
            d.wait_send()


def finish(n, out_v, gi_v, shard_v, gains_v, out, gi, dilated, point, own_in, own_mid, vin, vmid, sem):
    c, hid = vin.shape[0] * n, vmid.shape[0] * n
    me = lax.axis_index("seq")
    big = [pltpu.make_async_copy(a, b, sem.at[i]) for i, (a, b) in enumerate(
        ((out_v, out), (gi_v, gi), (shard_v.at[1:4], dilated), (shard_v.at[0], point)))]
    for d in big:
        d.start()
    for i, (lo, width, dst, hbm) in enumerate(((0, c, vin, own_in), (c, hid, vmid, own_mid))):
        size = width // n
        turned = pltpu.roll(gains_v[:, lo:lo + width], (width - me * size) % width, 1)
        dst[...] = jnp.sum(turned[:, 0:size], axis=0)
        small = pltpu.make_async_copy(dst, hbm, sem.at[4 + i])
        small.start()
        big.append(small)
    for d in big:
        d.wait()


def per_device(n, inputs, grad_out, w_dilated, w_point, gain_in, gain_mid, window_lengths):
    rows, c = inputs.shape
    hid = gain_mid.shape[0]
    levels = n.bit_length() - 1 if n & (n - 1) == 0 and c % (16 * n) == 0 else 0
    ext = rows + 2 * GH
    shard = (4, c // n, hid) if levels else (4, c, hid)
    slots = [(4, c >> (k + 1), hid) for k in range(levels)]
    sems = max(levels, 1)
    vmem = pltpu.VMEM
    dma = pltpu.SemaphoreType.DMA
    gain_slots = (sems, 8, c + hid)
    out, gin, shares, gains = pl.pallas_call(
        functools.partial(kernel, n, levels),
        out_shape=(
            jax.ShapeDtypeStruct((rows, c), BF16),
            jax.ShapeDtypeStruct((rows, c), BF16),
            jax.ShapeDtypeStruct(shard, F32),
            jax.ShapeDtypeStruct((8, c + hid), F32),
        ),
        in_specs=[pl.BlockSpec(memory_space=pltpu.HBM)] * 4 + [pl.BlockSpec(memory_space=vmem)] * 2
        + [pl.BlockSpec(memory_space=pltpu.SMEM)],
        out_specs=[pl.BlockSpec(memory_space=vmem)] * 4,
        scratch_shapes=[
            vmem((rows, c), BF16), vmem((rows, c), BF16), vmem(w_dilated.shape, BF16), vmem(w_point.shape, BF16),
            dma((4,)),
            vmem((2, XH, c), BF16), vmem((2, GH, c), BF16), vmem((rows + 2 * XH, c), BF16),
            vmem((rows, c), F32), vmem((ext, hid), F32), vmem((ext, hid), F32),
            vmem((ext, hid), BF16), vmem((ext, hid), BF16), vmem((3, rows, hid), BF16),
            vmem((rows, c), F32),
            vmem((n, c // n, rows) if levels else (8, 128), BF16), vmem((2, c, rows), BF16),
            vmem((ext, 1), F32), vmem((ext, 1), F32),
            vmem((4, c // 2, hid) if levels else (8, 128), F32), vmem((8, c + hid), F32),
            vmem(gain_slots, F32), vmem(gain_slots, F32),
            dma((4,)), dma((4,)), dma((sems,)), dma((sems,)), dma((4 * sems,)), dma((4 * sems,)),
        ] + [vmem(s, BF16) for s in slots] * 2,
        compiler_params=pltpu.CompilerParams(
            collective_id=0, has_side_effects=True, vmem_limit_bytes=48 * 2**20),
        cost_estimate=pl.CostEstimate(flops=12 * rows * c * hid, bytes_accessed=10 * rows * c, transcendentals=0),
    )(*[pltpu.with_memory_space_constraint(a, pltpu.HBM) for a in (
        inputs, grad_out, w_dilated, w_point, gain_in, gain_mid, window_lengths)])
    if levels:
        out, gin, dilated, point, own_in, own_mid = pl.pallas_call(
            functools.partial(finish, n),
            out_shape=(
                jax.ShapeDtypeStruct((rows, c), BF16),
                jax.ShapeDtypeStruct((rows, c), BF16),
                jax.ShapeDtypeStruct((3, c // n, hid), F32),
                jax.ShapeDtypeStruct((c // n, hid), F32),
                jax.ShapeDtypeStruct((c // n,), F32),
                jax.ShapeDtypeStruct((hid // n,), F32),
            ),
            in_specs=[pl.BlockSpec(memory_space=vmem)] * 4,
            out_specs=[pl.BlockSpec(memory_space=pltpu.HBM)] * 6,
            scratch_shapes=[vmem((c // n,), F32), vmem((hid // n,), F32), dma((6,))],
            compiler_params=pltpu.CompilerParams(vmem_limit_bytes=8 * 2**20),
        )(out, gin, shares, gains)
        return out, gin, dilated, point.T, own_in, own_mid
    shares = lax.psum_scatter(shares, "seq", scatter_dimension=1, tiled=True)
    total = jnp.sum(gains, axis=0)
    own_in = lax.psum_scatter(total[:c], "seq", scatter_dimension=0, tiled=True)
    own_mid = lax.psum_scatter(total[c:], "seq", scatter_dimension=0, tiled=True)
    return out, gin, shares[1:], shares[0].T, own_in, own_mid


def solution(mesh):
    rows = P(("groups", "seq"), None)
    vector = P(("groups", "seq"))
    return jax.shard_map(
        functools.partial(per_device, mesh.shape["seq"]),
        mesh=mesh,
        in_specs=(rows, rows, P(), P(), P(), P(), P("groups")),
        out_specs=(rows, rows, P("groups", "seq", None), P("groups", "seq"), vector, vector),
        check_vma=False,
    )
```

```python
import functools

import jax
import jax.numpy as jnp
from jax import lax
from jax.experimental import pallas as pl
from jax.experimental.pallas import tpu as pltpu
from jax.sharding import PartitionSpec as P

STEP = 38
XH = 96
GH = 48
EPS = 1e-06
K0 = 0.7978845608028654
K1 = 0.044715
F32 = jnp.float32
BF16 = jnp.bfloat16
NT = (((1,), (1,)), ((), ()))


def dot(a, b):
    return jnp.dot(a, b, preferred_element_type=F32)


def dot_nt(a, b):
    return lax.dot_general(a, b, NT, preferred_element_type=F32)


def gelu_parts(a):
    sq = a * a
    th = jnp.tanh(a * (K0 + (K0 * K1) * sq))
    half = 0.5 + 0.5 * th
    slope = half + a * (half * (1.0 - th)) * (K0 + (3.0 * K0 * K1) * sq)
    return a * half, slope


def scale_of(z):
    return lax.rsqrt(jnp.mean(z * z, axis=-1, keepdims=True) + EPS)


def fold(p):
    return jnp.sum(p.reshape(p.shape[0] // 8, 8, p.shape[1]), axis=0)


def kernel(n, levels, x_hbm, g_hbm, wd_hbm, wp_hbm, gin_ref, gmid_ref, len_ref,
           out_ref, gi_ref, shard_ref, gains_ref,
           x_ref, g_ref, wd_ref, wp_ref, ls, xh, gh, u_ref, gp_ref, h_ref, dv_ref, v_ref, dh_ref, dd_ref, du_ref,
           tmp, lt, mlo, mhi, acc, gacc, gs, gr, hs, hr, gss, grs, ss, rs, *bufs):
    rows, c = x_ref.shape
    hid = gmid_ref.shape[0]
    ext = rows + 2 * GH
    me = lax.axis_index("seq")
    left, right = (me + n - 1) % n, (me + 1) % n
    send, recv = bufs[:levels], bufs[levels:]
    bit = [(me // 2**k) % 2 for k in range(levels)]
    partner = [me + (1 - 2 * bit[k]) * 2**k for k in range(levels)]

    loads = [pltpu.make_async_copy(a, b, ls.at[i]) for i, (a, b) in enumerate(
        ((x_hbm, x_ref), (g_hbm, g_ref), (wp_hbm, wp_ref), (wd_hbm, wd_ref)))]
    for d in loads:
        d.start()
    def away(flips):
        return me + sum((1 - 2 * bit[k]) * 2**k for k in flips)

    rounds = []
    for k in range(0, levels, 2):
        rounds.append([(k,), (k + 1,), (k, k + 1)] if k + 1 < levels else [(k,)])
    barrier = pltpu.get_barrier_semaphore()
    peers = [left, right] + partner + [away(f) for r in rounds for f in r if len(f) == 2]
    for p in peers:
        pl.semaphore_signal(barrier, inc=1, device_id={"seq": p}, device_id_type=pl.DeviceIdType.MESH)
    pl.semaphore_wait(barrier, len(peers))

    def remote(src, dst, s, r, to):
        return pltpu.make_async_remote_copy(
            src_ref=src, dst_ref=dst, send_sem=s, recv_sem=r,
            device_id={"seq": to}, device_id_type=pl.DeviceIdType.MESH)

    up = [remote(x_hbm.at[rows - XH:rows], xh.at[0], hs.at[0], hr.at[0], right),
          remote(g_hbm.at[rows - GH:rows], gh.at[0], hs.at[1], hr.at[1], right)]
    down = [remote(x_hbm.at[0:XH], xh.at[1], hs.at[2], hr.at[2], left),
            remote(g_hbm.at[0:GH], gh.at[1], hs.at[3], hr.at[3], left)]

    @pl.when(me < n - 1)
    def _():
        for d in up:
            d.start()

    @pl.when(me > 0)
    def _():
        for d in down:
            d.start()

    @pl.when(me == 0)
    def _():
        xh[0] = jnp.zeros((XH, c), BF16)
        gh[0] = jnp.zeros((GH, c), BF16)

    @pl.when(me == n - 1)
    def _():
        xh[1] = jnp.zeros((XH, c), BF16)
        gh[1] = jnp.zeros((GH, c), BF16)

    gin = gin_ref[...].reshape(1, c)
    gmid = gmid_ref[...].reshape(1, hid)
    loads[0].wait()

    def act_own(i, carry):
        at = pl.multiple_of(i * 32, 32)
        z = x_ref[pl.ds(at, 32), :].astype(F32)
        u, slope = gelu_parts(z * scale_of(z) * gin)
        u_ref[pl.ds(XH + at, 32), :] = u.astype(BF16)
        gp_ref[pl.ds(at, 32), :] = slope
        return carry

    lax.fori_loop(0, rows // 128, lambda i, a: act_own(4 * i + 3, act_own(4 * i + 2, act_own(4 * i + 1, act_own(4 * i, a)))), 0)
    loads[1].wait()
    loads[2].wait()
    dv_ref[GH:GH + rows, :] = dot_nt(g_ref[...], wp_ref[...])

    count = len_ref.shape[0]
    lanes = -(-(count + 1) // 128) * 128
    lane = lax.broadcasted_iota(jnp.int32, (8, lanes), 1)
    b = jnp.zeros((8, lanes), jnp.int32)
    for w in range(count):
        b = b + jnp.where(lane > w, len_ref[w], 0)
    b = b[0:1, :]
    t = me * rows - GH + lax.broadcasted_iota(jnp.int32, (ext, b.shape[1]), 0)
    cut_lo = jnp.where((b > t - STEP) & (b <= t), 1.0, 0.0)
    cut_hi = jnp.where((b > t) & (b <= t + STEP), 1.0, 0.0)
    mlo[...] = 1.0 - jnp.max(cut_lo, axis=1, keepdims=True)
    mhi[...] = 1.0 - jnp.max(cut_hi, axis=1, keepdims=True)

    chunk = c // n if levels else c
    def transposed(j, value):
        if not levels:
            lt[j] = value.T
            return
        tmp[...] = value.T.reshape(n, chunk, rows)
        for s in range(n):
            at = 0
            for k in range(levels):
                flip = (s >> (levels - 1 - k)) & 1
                at = at + (1 - bit[k] if flip else bit[k]) * 2**k
            lt[j, s * chunk:(s + 1) * chunk] = tmp[at]

    transposed(0, g_ref[...])
    transposed(1, u_ref[XH:XH + rows, :])

    @pl.when(me > 0)
    def _():
        for d in up:
            d.wait_recv()

    @pl.when(me < n - 1)
    def _():
        for d in down:
            d.wait_recv()

    for side, base in ((0, 0), (1, XH + rows)):
        for i in range(XH // 32):
            z = xh[side, i * 32:(i + 1) * 32, :].astype(F32)
            u, _ = gelu_parts(z * scale_of(z) * gin)
            u_ref[base + i * 32:base + (i + 1) * 32, :] = u.astype(BF16)
    dv_ref[0:GH, :] = dot_nt(gh[0], wp_ref[...])
    dv_ref[GH + rows:ext, :] = dot_nt(gh[1], wp_ref[...])

    loads[3].wait()
    off = XH - GH
    tile = ext // 2
    for q in range(0, ext, tile):
        at = off + q
        low = dot(u_ref[at - STEP:at - STEP + tile, :], wd_ref[0])
        mid = dot(u_ref[at:at + tile, :], wd_ref[1])
        high = dot(u_ref[at + STEP:at + STEP + tile, :], wd_ref[2])
        h_ref[q:q + tile, :] = low * mlo[q:q + tile, :] + mid + high * mhi[q:q + tile, :]

    def middle(at, size):
        z = h_ref[pl.ds(at, size), :]
        r = scale_of(z)
        nz = z * r
        v, slope = gelu_parts(nz * gmid)
        da = dv_ref[pl.ds(at, size), :] * slope
        dn = da * gmid
        dz = r * (dn - nz * jnp.mean(dn * nz, axis=-1, keepdims=True))
        v_ref[pl.ds(at, size), :] = v.astype(BF16)
        dh_ref[pl.ds(at, size), :] = dz.astype(BF16)
        return da * nz

    middle(0, GH)
    middle(GH + rows, GH)
    gain_mid = lax.fori_loop(
        0, rows // 128,
        lambda i, a: a + fold(middle(pl.multiple_of(GH + i * 128, 16), 64)) + fold(middle(pl.multiple_of(GH + i * 128 + 64, 16), 64)),
        jnp.zeros((8, hid), F32))

    swap = levels == 4
    paths = [list(range(levels)) for _ in range(4)]
    if swap:
        paths[3] = [0, 2, 1, 3]
    step = {}

    def start(m, k):
        step[m, k] = remote(send[k].at[m], recv[k].at[m], ss.at[m * levels + k], rs.at[m * levels + k], partner[paths[m][k]])
        step[m, k].start()

    def share(m, left_t, right_m):
        if not levels:
            shard_ref[m] = dot(left_t[...], right_m)
            return
        half = c // 2
        quarter = half // 4
        places = [0, 2, 1, 3] if swap and m == 3 else [0, 1, 2, 3]
        far = dot(left_t[half:c, :], right_m).astype(BF16)
        for i, j in enumerate(places):
            send[0][m, i * quarter:(i + 1) * quarter, :] = far[j * quarter:(j + 1) * quarter, :]
        start(m, 0)
        near = dot(left_t[0:half, :], right_m)
        for i, j in enumerate(places):
            acc[m, i * quarter:(i + 1) * quarter, :] = near[j * quarter:(j + 1) * quarter, :]

    def advance(m, k):
        if not levels:
            return
        size = c >> (k + 1)
        step[m, k].wait_recv()
        if k == levels - 1:
            shard_ref[m] = acc[m, 0:size, :] + recv[k][m].astype(F32)
            return
        half = size // 2
        send[k + 1][m] = (acc[m, half:size, :] + recv[k][m, half:size, :].astype(F32)).astype(BF16)
        start(m, k + 1)
        acc[m, 0:half, :] = acc[m, 0:half, :] + recv[k][m, 0:half, :].astype(F32)

    def wave(i):
        for m in range(4):
            if 0 <= i - m < levels:
                advance(m, i - m)

    share(0, lt.at[0], v_ref[GH:GH + rows, :])
    own = slice(GH, GH + rows)
    dd_ref[0] = (dh_ref[GH + STEP:GH + STEP + rows, :].astype(F32) * mhi[own, :]).astype(BF16)
    share(1, lt.at[1], dd_ref[0])
    wave(0)
    dd_ref[1] = dh_ref[own, :]
    share(2, lt.at[1], dd_ref[1])
    if levels:
        advance(1, 0)
    dd_ref[2] = (dh_ref[GH - STEP:GH - STEP + rows, :].astype(F32) * mlo[own, :]).astype(BF16)
    share(3, lt.at[1], dd_ref[2])
    if levels:
        advance(2, 0)

    def cotangent(q, size):
        du_ref[q:q + size, :] = (dot_nt(dd_ref[0, q:q + size, :], wd_ref[0])
                                 + dot_nt(dd_ref[1, q:q + size, :], wd_ref[1])
                                 + dot_nt(dd_ref[2, q:q + size, :], wd_ref[2]))

    def back(i, a):
        at = pl.multiple_of(i * 32, 32)
        z = x_ref[pl.ds(at, 32), :].astype(F32)
        r = scale_of(z)
        nz = z * r
        da = du_ref[pl.ds(at, 32), :] * gp_ref[pl.ds(at, 32), :]
        dn = da * gin
        dz = r * (dn - nz * jnp.mean(dn * nz, axis=-1, keepdims=True))
        gi_ref[pl.ds(at, 32), :] = (g_ref[pl.ds(at, 32), :].astype(F32) + dz).astype(BF16)
        return a + fold(da * nz)

    gains = {}

    def gain_start(r):
        if r < len(rounds):
            gs[r] = gacc[...]
            for i, f in enumerate(rounds[r]):
                j = 3 * r + i
                gains[r, i] = remote(gs.at[r], gr.at[j], gss.at[j], grs.at[j], away(f))
                gains[r, i].start()

    def gain_end(r):
        if r < len(rounds):
            for i in range(len(rounds[r])):
                gains[r, i].wait_recv()
                gacc[...] = gacc[...] + gr[3 * r + i]

    def output(q, size):
        y = dot(v_ref[GH + q:GH + q + size, :], wp_ref[...])
        out_ref[q:q + size, :] = (x_ref[q:q + size, :].astype(F32) + y).astype(BF16)

    def back_two(i, a):
        return back(4 * i + 3, back(4 * i + 2, back(4 * i + 1, back(4 * i, a))))

    half_rows = rows // 2
    quarter_rows = rows // 4
    advanced = {(0, 0), (1, 0), (2, 0)}

    def go(*pairs):
        for m, k in pairs:
            if k < levels and (m, k) not in advanced:
                advance(m, k)
                advanced.add((m, k))

    gain_in = jnp.zeros((8, c), F32)
    cotangent(0, half_rows)
    go((3, 0))
    cotangent(half_rows, half_rows)
    go((0, 1))
    gain_in = lax.fori_loop(0, half_rows // 128, back_two, gain_in)
    go((3, 1), (1, 1), (0, 2))
    gain_in = lax.fori_loop(half_rows // 128, rows // 128, back_two, gain_in)
    if not levels:
        gains_ref[:, 0:c] = gain_in
        gains_ref[:, c:c + hid] = gain_mid
    else:
        gacc[:, 0:c] = jnp.sum(gain_in, axis=0, keepdims=True)
        gacc[:, c:c + hid] = jnp.sum(gain_mid, axis=0, keepdims=True)
    gain_start(0)
    go((2, 1))
    output(0, half_rows)
    go((1, 2), (0, 3))
    gain_end(0)
    gain_start(1)
    go((3, 2))
    output(half_rows, half_rows)
    go(*[(m, i - m) for i in range(levels + 3) for m in range(4) if 0 <= i - m < levels])
    if levels:
        gain_end(1)
        first = lax.broadcasted_iota(jnp.int32, (8, c + hid), 0) == 0
        gains_ref[...] = jnp.where(first, gacc[...], 0.0)
        for d in list(step.values()) + list(gains.values()):
            d.wait_send()

    @pl.when(me < n - 1)
    def _():
        for d in up:
            d.wait_send()

    @pl.when(me > 0)
    def _():
        for d in down:
            d.wait_send()


def finish(n, out_v, gi_v, shard_v, gains_v, out, gi, dilated, point, own_in, own_mid, vin, vmid, sem):
    c, hid = vin.shape[0] * n, vmid.shape[0] * n
    me = lax.axis_index("seq")
    big = [pltpu.make_async_copy(a, b, sem.at[i]) for i, (a, b) in enumerate(
        ((out_v, out), (gi_v, gi), (shard_v.at[1:4], dilated), (shard_v.at[0], point)))]
    for d in big:
        d.start()
    for i, (lo, width, dst, hbm) in enumerate(((0, c, vin, own_in), (c, hid, vmid, own_mid))):
        size = width // n
        turned = pltpu.roll(gains_v[:, lo:lo + width], (width - me * size) % width, 1)
        dst[...] = jnp.sum(turned[:, 0:size], axis=0)
        small = pltpu.make_async_copy(dst, hbm, sem.at[4 + i])
        small.start()
        big.append(small)
    for d in big:
        d.wait()


def per_device(n, inputs, grad_out, w_dilated, w_point, gain_in, gain_mid, window_lengths):
    rows, c = inputs.shape
    hid = gain_mid.shape[0]
    levels = n.bit_length() - 1 if n & (n - 1) == 0 and c % (16 * n) == 0 else 0
    ext = rows + 2 * GH
    shard = (4, c // n, hid) if levels else (4, c, hid)
    slots = [(4, c >> (k + 1), hid) for k in range(levels)]
    sems = max(levels, 1)
    vmem = pltpu.VMEM
    dma = pltpu.SemaphoreType.DMA
    swaps = 3 * -(-sems // 2)
    out, gin, shares, gains = pl.pallas_call(
        functools.partial(kernel, n, levels),
        out_shape=(
            jax.ShapeDtypeStruct((rows, c), BF16),
            jax.ShapeDtypeStruct((rows, c), BF16),
            jax.ShapeDtypeStruct(shard, F32),
            jax.ShapeDtypeStruct((8, c + hid), F32),
        ),
        in_specs=[pl.BlockSpec(memory_space=pltpu.HBM)] * 4 + [pl.BlockSpec(memory_space=vmem)] * 2
        + [pl.BlockSpec(memory_space=pltpu.SMEM)],
        out_specs=[pl.BlockSpec(memory_space=vmem)] * 4,
        scratch_shapes=[
            vmem((rows, c), BF16), vmem((rows, c), BF16), vmem(w_dilated.shape, BF16), vmem(w_point.shape, BF16),
            dma((4,)),
            vmem((2, XH, c), BF16), vmem((2, GH, c), BF16), vmem((rows + 2 * XH, c), BF16),
            vmem((rows, c), F32), vmem((ext, hid), F32), vmem((ext, hid), F32),
            vmem((ext, hid), BF16), vmem((ext, hid), BF16), vmem((3, rows, hid), BF16),
            vmem((rows, c), F32),
            vmem((n, c // n, rows) if levels else (8, 128), BF16), vmem((2, c, rows), BF16),
            vmem((ext, 1), F32), vmem((ext, 1), F32),
            vmem((4, c // 2, hid) if levels else (8, 128), F32), vmem((1, c + hid), F32),
            vmem((swaps, 1, c + hid), F32), vmem((swaps, 1, c + hid), F32),
            dma((4,)), dma((4,)), dma((swaps,)), dma((swaps,)), dma((4 * sems,)), dma((4 * sems,)),
        ] + [vmem(s, BF16) for s in slots] * 2,
        compiler_params=pltpu.CompilerParams(
            collective_id=0, has_side_effects=True, vmem_limit_bytes=48 * 2**20),
        cost_estimate=pl.CostEstimate(flops=12 * rows * c * hid, bytes_accessed=10 * rows * c, transcendentals=0),
    )(*[pltpu.with_memory_space_constraint(a, pltpu.HBM) for a in (
        inputs, grad_out, w_dilated, w_point, gain_in, gain_mid, window_lengths)])
    if levels:
        out, gin, dilated, point, own_in, own_mid = pl.pallas_call(
            functools.partial(finish, n),
            out_shape=(
                jax.ShapeDtypeStruct((rows, c), BF16),
                jax.ShapeDtypeStruct((rows, c), BF16),
                jax.ShapeDtypeStruct((3, c // n, hid), F32),
                jax.ShapeDtypeStruct((c // n, hid), F32),
                jax.ShapeDtypeStruct((c // n,), F32),
                jax.ShapeDtypeStruct((hid // n,), F32),
            ),
            in_specs=[pl.BlockSpec(memory_space=vmem)] * 4,
            out_specs=[pl.BlockSpec(memory_space=pltpu.HBM)] * 6,
            scratch_shapes=[vmem((c // n,), F32), vmem((hid // n,), F32), dma((6,))],
            compiler_params=pltpu.CompilerParams(vmem_limit_bytes=8 * 2**20),
        )(out, gin, shares, gains)
        return out, gin, dilated, point.T, own_in, own_mid
    shares = lax.psum_scatter(shares, "seq", scatter_dimension=1, tiled=True)
    total = jnp.sum(gains, axis=0)
    own_in = lax.psum_scatter(total[:c], "seq", scatter_dimension=0, tiled=True)
    own_mid = lax.psum_scatter(total[c:], "seq", scatter_dimension=0, tiled=True)
    return out, gin, shares[1:], shares[0].T, own_in, own_mid


def solution(mesh):
    rows = P(("groups", "seq"), None)
    vector = P(("groups", "seq"))
    return jax.shard_map(
        functools.partial(per_device, mesh.shape["seq"]),
        mesh=mesh,
        in_specs=(rows, rows, P(), P(), P(), P(), P("groups")),
        out_specs=(rows, rows, P("groups", "seq", None), P("groups", "seq"), vector, vector),
        check_vma=False,
    )
```
